256 devices in a mesh: tile: 64 (over z_hi, x, y, core), agent: 4 (over z_lo).
Axes of the slice: x: 4, y: 4, z: 8 (z_hi: 2, z_lo: 4; z = z_hi * 4 + z_lo), core: 2. Of those that a mesh axis runs over, the one named last changes fastest.
Arguments:
- view_tile: bfloat16 [16, 64, 768, 1024], P('agent', 'tile'), may hold values from -0.0234375 to 0.0234375
- block_mask: int32 [16, 64, 6, 8], P('agent', 'tile'), may hold values 0 or 1
- sinogram: float32 [16, 32, 768], P('agent'), may hold values from -24 to 24
- bin_weight: float32 [16, 32, 768], P('agent'), may hold values from 0.2 to 0.6
- model_state: float32 [64, 32, 1024], P('tile', 'agent'), may hold values from -6 to 6
- planar_state: float32 [64, 32, 1024], P('tile', 'agent'), may hold values from -6 to 6
- sagittal_state: float32 [64, 32, 1024], P('tile', 'agent'), may hold values from -6 to 6
- planar_in: float32 [9, 16], replicated, may hold values from -3 to 3
- planar_mid: float32 [3, 9, 16, 16], replicated, may hold values from -0.75 to 0.75
- planar_out: float32 [9, 16], replicated, may hold values from -0.5 to 0.5
- sagittal_in: float32 [9, 16], replicated, may hold values from -3 to 3
- sagittal_mid: float32 [3, 9, 16, 16], replicated, may hold values from -0.75 to 0.75
- sagittal_out: float32 [9, 16], replicated, may hold values from -0.5 to 0.5
Outputs:
- model_next: float32 [64, 32, 1024], P('tile', 'agent')
- planar_next: float32 [64, 32, 1024], P('tile', 'agent')
- sagittal_next: float32 [64, 32, 1024], P('tile', 'agent')
The draws below stay inside these ranges and needn't reach their ends.
All inputs are finite; a program needn't handle non-finite values. No bound on the sum of `block_mask` on one device may be relied on, other than what follows from the above.
Results may differ from the reference program's by a relative error of at most 0.0055.
Values may be sent and summed in bfloat16 or wider, within the bound.
No kernel may reach another device: no remote copies, remote signals or barrier semaphores. Data moves between devices by JAX's collectives and lax.ppermute only.
A program may use at most 128 MiB of HBM per device.

```python
import math
import jax
import jax.numpy as jnp
from jax import lax

BINS = 768
TILE_VOX = 1024
BLOCK = 128
PX = 8
SLICES = 32
HIDDEN_SIZE = 16
MID = 3
GRAD_STEPS = 2
TAPS = 9
TILES = 64
VIEWS = 16
NX = 512
NY = 128


def place_ends(values, stream_key, least, largest):
    longest = values.shape.index(max(values.shape))
    spots = []
    for shift in (0, 1):
        where = [jax.random.randint(jax.random.fold_in(stream_key, axis), (), 0, length) for axis, length in enumerate(values.shape)]
        where[longest] = (where[longest] + shift) % values.shape[longest]
        spots.append(tuple(where))
    return values.at[spots[0]].set(least).at[spots[1]].set(largest)


def block_scale(stream_key, shape, shards, least, high):
    level = 1.0
    for axis_at, shards_of in shards:
        draws = jax.random.uniform(jax.random.fold_in(jax.random.fold_in(stream_key, 6), axis_at), (shards_of,), jnp.float32, least / len(shards), high / len(shards))
        level = level * jnp.repeat(jnp.exp(draws), shape[axis_at] // shards_of).reshape((-1,) + (1,) * (len(shape) - 1 - axis_at))
    return level


def centred(own_key, extent, spread, bound, pieces=(), kind=jnp.bfloat16):
    drawn = jax.random.normal(own_key, extent, jnp.float32) * spread
    if len(pieces) > 0:
        drawn = block_scale(own_key, extent, pieces, -0.22, 0.18) * drawn
    return jnp.clip(drawn, min=-bound, max=bound).astype(kind)


def setup_inputs(seed: int = 0) -> dict:
    seeds = jax.random.split(jax.random.key(seed), 14)
    view_tile = centred(seeds[0], (VIEWS, TILES, BINS, TILE_VOX), (TILE_VOX * TILES) ** -0.5, 0.0234375, ((0, 4), (1, 64)))
    block_mask = place_ends((jax.random.randint(seeds[1], (VIEWS, TILES, BINS // BLOCK, TILE_VOX // BLOCK), 0, 3) < 2).astype(jnp.int32), jax.random.fold_in(seeds[1], 1), 0, 1)
    sinogram = centred(seeds[2], (VIEWS, SLICES, BINS), 4.0, 24.0, ((0, 4),), jnp.float32)
    bin_weight = jnp.clip(jnp.exp(math.log(0.6) - 1.0986123 * jax.random.uniform(seeds[3], (VIEWS, SLICES, BINS), jnp.float32) ** block_scale(seeds[3], (VIEWS, SLICES, BINS), ((0, 4),), -0.2, 0.2)), 0.2, 0.6)
    model_state = centred(seeds[4], (TILES, SLICES, TILE_VOX), 1.0, 6.0, ((0, 64), (1, 4)), jnp.float32)
    planar_state = centred(seeds[5], (TILES, SLICES, TILE_VOX), 1.0, 6.0, ((0, 64), (1, 4)), jnp.float32)
    sagittal_state = centred(seeds[6], (TILES, SLICES, TILE_VOX), 1.0, 6.0, ((0, 64), (1, 4)), jnp.float32)
    planar_in = centred(seeds[7], (TAPS, HIDDEN_SIZE), (TAPS // 2) ** -0.5, 3.0, (), jnp.float32)
    planar_mid = centred(seeds[8], (MID, TAPS, HIDDEN_SIZE, HIDDEN_SIZE), (TAPS * HIDDEN_SIZE // 2) ** -0.5, 0.75, (), jnp.float32)
    planar_out = centred(seeds[9], (TAPS, HIDDEN_SIZE), (TAPS * HIDDEN_SIZE) ** -0.5, 0.5, (), jnp.float32)
    sagittal_in = centred(seeds[10], (TAPS, HIDDEN_SIZE), (TAPS // 2) ** -0.5, 3.0, (), jnp.float32)
    sagittal_mid = centred(seeds[11], (MID, TAPS, HIDDEN_SIZE, HIDDEN_SIZE), (TAPS * HIDDEN_SIZE // 2) ** -0.5, 0.75, (), jnp.float32)
    sagittal_out = centred(seeds[12], (TAPS, HIDDEN_SIZE), (TAPS * HIDDEN_SIZE) ** -0.5, 0.5, (), jnp.float32)
    return dict(view_tile=view_tile, block_mask=block_mask, sinogram=sinogram, bin_weight=bin_weight, model_state=model_state, planar_state=planar_state, sagittal_state=sagittal_state, planar_in=planar_in, planar_mid=planar_mid, planar_out=planar_out, sagittal_in=sagittal_in, sagittal_mid=sagittal_mid, sagittal_out=sagittal_out)


step_size = 0.5
prox_weight = 1.0
relax_rate = 0.5
share_model = 0.5
share_plane = 0.25
share_side = 0.25
highest = lax.Precision.HIGHEST


def blocked(matrix, pattern):
    leading = matrix.shape[:-2]
    rows_in = matrix.shape[-2]
    cols_in = matrix.shape[-1]
    row_blocks = pattern.shape[-2]
    col_blocks = pattern.shape[-1]
    tiled_grid = matrix.reshape(leading + (row_blocks, rows_in // row_blocks, col_blocks, cols_in // col_blocks))
    keeper = pattern.astype(matrix.dtype)[..., :, None, :, None]
    return (tiled_grid * keeper).reshape(matrix.shape)


def convolve(activity, kernel):
    span_rows = activity.shape[2] - 2
    span_cols = activity.shape[3] - 2
    summed = jnp.zeros((kernel.shape[1], activity.shape[1], span_rows, span_cols), jnp.float32)
    for offset in range(9):
        row_off = offset // 3
        col_off = offset % 3
        window = activity[:, :, row_off:row_off + span_rows, col_off:col_off + span_cols]
        summed = summed + jnp.einsum("oc,cbhw->obhw", kernel[offset], window, precision=highest)
    return summed


def pad_both(activity):
    return jnp.pad(activity, ((0, 0), (0, 0), (1, 1), (1, 1)))


def kernels(first_in, middle, last_out):
    return [first_in[:, :, None]] + [middle[member] for member in range(middle.shape[0])] + [last_out[:, None, :]]


def denoise(volume, first_in, middle, last_out):
    kernel_list = kernels(first_in, middle, last_out)
    current = volume[None]
    for position, kernel in enumerate(kernel_list):
        current = convolve(pad_both(current), kernel)
        if position + 1 < len(kernel_list):
            current = jax.nn.relu(current)
    return volume - current[0]


def to_volume(state):
    return state.reshape(TILES, SLICES, PX, NY).transpose(1, 0, 2, 3).reshape(SLICES, NX, NY)


def from_volume(volume):
    return volume.reshape(SLICES, TILES, PX, NY).transpose(1, 0, 2, 3).reshape(TILES, SLICES, PX * NY)


def reference(view_tile, block_mask, sinogram, bin_weight, model_state, planar_state, sagittal_state, planar_in, planar_mid, planar_out, sagittal_in, sagittal_mid, sagittal_out):
    guess = model_state
    for iteration in range(GRAD_STEPS):
        guess_low = lax.optimization_barrier(guess.astype(jnp.bfloat16)).astype(jnp.float32)

        def forward(operands):
            matrix, pattern = operands
            masked = blocked(matrix, pattern).astype(jnp.float32)
            return jnp.einsum("tsk,tbk->sb", guess_low, masked, precision=highest)

        projection = lax.map(forward, (view_tile, block_mask))
        misfit = lax.optimization_barrier((bin_weight * (projection - sinogram)).astype(jnp.bfloat16)).astype(jnp.float32)

        def backward(running, triple):
            matrix, pattern, residue = triple
            masked = blocked(matrix, pattern).astype(jnp.float32)
            return running + jnp.einsum("sb,tbk->tsk", residue, masked, precision=highest), None

        gradient, leftover = lax.scan(backward, jnp.zeros(guess.shape, jnp.float32), (view_tile, block_mask, misfit))
        guess = guess - step_size * (gradient + prox_weight * (guess - model_state))
    model_image = guess
    planar_image = from_volume(denoise(to_volume(planar_state), planar_in, planar_mid, planar_out))
    side_volume = to_volume(sagittal_state).transpose(1, 0, 2)
    sagittal_image = from_volume(denoise(side_volume, sagittal_in, sagittal_mid, sagittal_out).transpose(1, 0, 2))
    reflect_model = 2.0 * model_image - model_state
    reflect_plane = 2.0 * planar_image - planar_state
    reflect_side = 2.0 * sagittal_image - sagittal_state
    consensus = share_model * reflect_model + share_plane * reflect_plane + share_side * reflect_side
    model_next = (1.0 - relax_rate) * model_state + relax_rate * (2.0 * consensus - reflect_model)
    planar_next = (1.0 - relax_rate) * planar_state + relax_rate * (2.0 * consensus - reflect_plane)
    sagittal_next = (1.0 - relax_rate) * sagittal_state + relax_rate * (2.0 * consensus - reflect_side)
    return (model_next, planar_next, sagittal_next)
```

```python
import jax
import jax.numpy as jnp
from jax import lax
from jax.sharding import Mesh, PartitionSpec as P

PX = 8
GRAD_STEPS = 2
HALO = 5
PLANE = ("x", "y", "core")
TILE = ("zh",) + PLANE

highest = lax.Precision.HIGHEST


def blocked(matrix, pattern):
    leading = matrix.shape[:-2]
    rows_in, cols_in = matrix.shape[-2:]
    row_blocks, col_blocks = pattern.shape[-2:]
    grid = matrix.reshape(
        leading + (row_blocks, rows_in // row_blocks, col_blocks, cols_in // col_blocks)
    )
    keeper = pattern.astype(matrix.dtype)[..., :, None, :, None]
    return (grid * keeper).reshape(matrix.shape)


def line(count, shift):
    return [(i, i + shift) for i in range(count) if 0 <= i + shift < count]


def with_halo(block, axis, count):
    low = lax.ppermute(block[:, -HALO:], axis, line(count, 1))
    high = lax.ppermute(block[:, :HALO], axis, line(count, -1))
    return jnp.concatenate([low, block, high], axis=1)


def denoise(field, first_in, middle, last_out, at, count):
    kernels = (
        [first_in[:, :, None]] + [middle[i] for i in range(middle.shape[0])] + [last_out[:, None, :]]
    )
    own = field.shape[1] - 2 * HALO
    current = field[None]
    for position, kernel in enumerate(kernels):
        rows = current.shape[2] - 2
        padded = jnp.pad(current, ((0, 0), (0, 0), (0, 0), (1, 1)))
        summed = 0.0
        for tap in range(9):
            a, e = divmod(tap, 3)
            window = padded[:, :, a : a + rows, e : e + current.shape[3]]
            summed = summed + jnp.einsum("oc,cbhw->obhw", kernel[tap], window, precision=highest)
        current = summed
        if position + 1 < len(kernels):
            current = jax.nn.relu(current)
            reach = (rows - own) // 2
            row = lax.broadcasted_iota(jnp.int32, (1, 1, rows, 1), 2) + at * own - reach
            current = jnp.where((row >= 0) & (row < count * own), current, 0.0)
    return field[:, HALO:-HALO] - current[0]


def body(
    view_tile,
    block_mask,
    sinogram,
    bin_weight,
    model_state,
    planar_state,
    sagittal_state,
    planar_in,
    planar_mid,
    planar_out,
    sagittal_in,
    sagittal_mid,
    sagittal_out,
):
    agents = lax.axis_size("agent")
    me = lax.axis_index("agent")
    tiles = lax.axis_size(TILE)
    spread = lax.axis_size(PLANE)
    spot = lax.axis_index(PLANE)
    own = model_state.shape[1]
    voxels = model_state.shape[2]
    views, _, bins, _ = view_tile.shape
    slices = own * agents
    tiles_all = views * slices * bins // 1024
    per = tiles_all // spread

    masked = blocked(view_tile[:, 0], block_mask[:, 0])

    def to_tiles(values):
        return values.reshape(views, slices // 8, 8, bins // 128, 128).transpose(0, 1, 3, 2, 4).reshape(
            spread, per, 8, 128
        )

    def from_tiles(values):
        return values.reshape(views, slices // 8, bins // 128, 8, 128).transpose(0, 1, 3, 2, 4).reshape(
            views, slices, bins
        )

    sino = lax.dynamic_index_in_dim(to_tiles(sinogram), spot, 0, keepdims=False)
    weight = lax.dynamic_index_in_dim(to_tiles(bin_weight), spot, 0, keepdims=False)

    def gather_slices(low):
        parts = [low] + [
            lax.ppermute(low, "agent", [(i, i ^ k) for i in range(agents)]) for k in range(1, agents)
        ]
        stacked = jnp.stack(parts)
        order = jnp.arange(agents) ^ me
        return stacked[order].reshape(slices, voxels)

    def scatter_slices(partial):
        low = partial.astype(jnp.bfloat16).reshape(agents, own, voxels)
        total = lax.dynamic_index_in_dim(low, me, 0, keepdims=False).astype(jnp.float32)
        for k in range(1, agents):
            part = lax.dynamic_index_in_dim(low, me ^ k, 0, keepdims=False)
            total = total + lax.ppermute(part, "agent", [(i, i ^ k) for i in range(agents)]).astype(
                jnp.float32
            )
        return total

    anchor = model_state[0]
    guess = anchor
    for _ in range(GRAD_STEPS):
        low = gather_slices(guess.astype(jnp.bfloat16))
        partial = jnp.einsum("sk,vbk->vsb", low, masked, preferred_element_type=jnp.float32)
        sent = to_tiles(partial.astype(jnp.bfloat16))
        got = lax.all_to_all(sent, PLANE, 0, 0)
        half = got.astype(jnp.float32).sum(axis=0)
        other = lax.ppermute(half, "zh", [(0, 1), (1, 0)])
        misfit = (weight * ((half + other) - sino)).astype(jnp.bfloat16)
        spreaded = jnp.broadcast_to(misfit[None], (spread, per, 8, 128))
        misfit = from_tiles(lax.all_to_all(spreaded, PLANE, 0, 0))
        gradient = scatter_slices(
            jnp.einsum("vsb,vbk->sk", misfit, masked, preferred_element_type=jnp.float32)
        )
        guess = guess - 0.5 * (gradient + (guess - anchor))
    model_image = guess[None]

    plane = with_halo(planar_state[0].reshape(own, PX, voxels // PX), TILE, tiles)
    plane = denoise(plane, planar_in, planar_mid, planar_out, lax.axis_index(TILE), tiles)
    planar_image = plane.reshape(1, own, voxels)
    side = sagittal_state[0].reshape(own, PX, voxels // PX).transpose(1, 0, 2)
    side = with_halo(side, "agent", agents)
    side = denoise(side, sagittal_in, sagittal_mid, sagittal_out, me, agents)
    sagittal_image = side.transpose(1, 0, 2).reshape(1, own, voxels)

    reflect_model = 2.0 * model_image - model_state
    reflect_plane = 2.0 * planar_image - planar_state
    reflect_side = 2.0 * sagittal_image - sagittal_state
    consensus = 0.5 * reflect_model + 0.25 * reflect_plane + 0.25 * reflect_side
    model_next = 0.5 * model_state + 0.5 * (2.0 * consensus - reflect_model)
    planar_next = 0.5 * planar_state + 0.5 * (2.0 * consensus - reflect_plane)
    sagittal_next = 0.5 * sagittal_state + 0.5 * (2.0 * consensus - reflect_side)
    return (model_next, planar_next, sagittal_next)


def solution(mesh):
    fine = Mesh(mesh.devices.reshape(2, 4, 4, 2, 4), TILE + ("agent",))
    return jax.shard_map(
        body,
        mesh=fine,
        in_specs=(
            P("agent", TILE, None, None),
            P("agent", TILE, None, None),
            P("agent", None, None),
            P("agent", None, None),
            P(TILE, "agent", None),
            P(TILE, "agent", None),
            P(TILE, "agent", None),
            P(),
            P(),
            P(),
            P(),
            P(),
            P(),
        ),
        out_specs=(P(TILE, "agent", None),) * 3,
        check_vma=False,
    )
```

```python
import jax
import jax.numpy as jnp
from jax import lax
from jax.experimental import pallas as pl
from jax.experimental.pallas import tpu as pltpu
from jax.sharding import Mesh, PartitionSpec as P


PX = 8
HALO = 5
LANES = 128
SPLIT = 2
PLANE = ("x", "y", "core")
TILE = ("zh",) + PLANE

bf16 = jnp.bfloat16
f32 = jnp.float32
VMEM = pl.BlockSpec(memory_space=pltpu.VMEM)
SMEM = pl.BlockSpec(memory_space=pltpu.SMEM)
HBM = pl.BlockSpec(memory_space=pltpu.HBM)


def params(mebibytes, axes=0):
    return pltpu.CompilerParams(
        vmem_limit_bytes=mebibytes << 20, dimension_semantics=("arbitrary",) * axes or None
    )


def onchip(value):
    return pltpu.with_memory_space_constraint(value, pltpu.VMEM)


def fetch(source, target, sems):
    views, bins, _ = target.shape
    rows = bins // SPLIT
    copies = []
    for v in range(views):
        for h in range(SPLIT):
            copy = pltpu.make_async_copy(
                source.at[v, pl.ds(h * rows, rows)],
                target.at[v, pl.ds(h * rows, rows)],
                sems.at[v * SPLIT + h],
            )
            copy.start()
            copies.append((v, h * rows, copy))
    return copies


def offchip(value):
    return pltpu.with_memory_space_constraint(value, pltpu.HBM)


def mask_blocks(view_tile, mask):
    views, _, bins, voxels = view_tile.shape
    rows = bins // SPLIT

    def kernel(mask_ref, view_ref, chip_ref, sems):
        for v, first, copy in fetch(view_ref.at[:, 0], chip_ref, sems):
            copy.wait()
            for j in range(first, first + rows, LANES):
                for k in range(voxels // LANES):
                    keep = jnp.full((16, LANES), mask_ref[v, 0, j // LANES, k].astype(f32)).astype(bf16)
                    at = (v, slice(j, j + LANES), slice(k * LANES, (k + 1) * LANES))
                    block = chip_ref[at].reshape(8, 16, LANES) * keep[None]
                    chip_ref[at] = block.reshape(LANES, LANES)

    return pl.pallas_call(
        kernel,
        out_shape=pltpu.VMEM((views, bins, voxels), bf16),
        in_specs=[SMEM, HBM],
        out_specs=VMEM,
        scratch_shapes=[pltpu.SemaphoreType.DMA((views * SPLIT,))],
        compiler_params=params(16),
        name="mask_blocks",
    )(mask, offchip(view_tile))


def project_tiles(low, matrix_ref, out_ref):
    views, bins, _ = matrix_ref.shape
    groups, blocks = low.shape[0] // 8, bins // LANES
    for v in range(views):
        result = lax.dot_general(
            low, matrix_ref[v], (((1,), (1,)), ((), ())), preferred_element_type=f32
        ).astype(bf16)
        for g in range(groups):
            for j in range(blocks):
                out_ref[(v * groups + g) * blocks + j] = result[8 * g : 8 * g + 8, j * LANES : (j + 1) * LANES]


def project_first(parts, matrix, me):
    own, voxels = parts[0].shape
    groups = len(parts)
    views, bins, _ = matrix.shape

    def kernel(me_ref, *refs):
        part_refs, (matrix_ref, out_ref, anchor_ref, main_ref, sems) = refs[:groups], refs[groups:]
        copies = fetch(matrix_ref, main_ref, sems)
        for k in range(groups):
            first = pl.multiple_of(jnp.bitwise_xor(me_ref[0], k) * own, own)
            anchor_ref[pl.ds(first, own), :] = part_refs[k][...].astype(f32)
        project_tiles(anchor_ref[...].astype(bf16), matrix_ref, out_ref)
        for *_, copy in copies:
            copy.wait()

    return pl.pallas_call(
        kernel,
        out_shape=[
            jax.ShapeDtypeStruct((views * groups * bins // LANES, own, LANES), bf16),
            jax.ShapeDtypeStruct((groups * own, voxels), f32),
            pltpu.HBM(matrix.shape, bf16),
        ],
        in_specs=[SMEM] + [VMEM] * (groups + 1),
        out_specs=[VMEM, VMEM, HBM],
        scratch_shapes=[pltpu.SemaphoreType.DMA((views * SPLIT,))],
        compiler_params=params(16),
        name="project_first",
    )(me, *[onchip(p) for p in parts], onchip(matrix))


def project_next(anchor, pieces, matrix, me):
    slices, voxels = anchor.shape
    views, bins, _ = matrix.shape
    own = 8
    count = len(pieces)

    def kernel(me_ref, anchor_ref, *refs):
        piece_refs, (matrix_ref, out_ref, own_ref, gradient_ref) = refs[:count], refs[count:]
        gradient = piece_refs[0][...]
        for ref in piece_refs[1:]:
            gradient = gradient + ref[...].astype(f32)
        gradient_ref[...] = gradient
        low = (anchor_ref[...] - 0.5 * gradient).astype(bf16)
        own_ref[...] = gradient_ref[pl.ds(pl.multiple_of(me_ref[0] * own, own), own), :]
        project_tiles(low, matrix_ref, out_ref)

    return pl.pallas_call(
        kernel,
        out_shape=[
            jax.ShapeDtypeStruct((views * slices // own * bins // LANES, own, LANES), bf16),
            jax.ShapeDtypeStruct((own, voxels), f32),
        ],
        in_specs=[SMEM] + [VMEM] * (count + 2),
        out_specs=[VMEM, VMEM],
        scratch_shapes=[pltpu.VMEM((slices, voxels), f32)],
        compiler_params=params(16),
        name="project_next",
    )(me, onchip(anchor), *[onchip(p) for p in pieces], onchip(matrix))


def back_project(misfit, matrix, me, groups, whole):
    views, bins, voxels = matrix.shape
    own = misfit.shape[1]
    blocks = bins // LANES
    rows = bins // SPLIT

    def kernel(me_ref, misfit_ref, matrix_ref, *refs):
        *outs, chip_ref, sems = refs if whole else refs[:-3] + refs[-2:]
        total = None
        for v, first, copy in fetch(matrix_ref, chip_ref, sems):
            left = jnp.concatenate(
                [
                    jnp.concatenate(
                        [
                            misfit_ref[(v * groups + g) * blocks + j].astype(f32)
                            for j in range(first // LANES, (first + rows) // LANES)
                        ],
                        axis=1,
                    )
                    for g in range(groups)
                ],
                axis=0,
            ).astype(bf16)
            copy.wait()
            part = jnp.dot(left, chip_ref[v, first : first + rows, :], preferred_element_type=f32)
            total = part if total is None else total + part
        if whole:
            outs[0][...] = total
            outs[1][...] = total.astype(bf16)
        else:
            total_ref = refs[-3]
            total_ref[...] = total
            for k in range(groups):
                first = pl.multiple_of(jnp.bitwise_xor(me_ref[0], k) * own, own)
                outs[k][...] = total_ref[pl.ds(first, own), :].astype(outs[k].dtype)

    if whole:
        outs = [jax.ShapeDtypeStruct((groups * own, voxels), t) for t in (f32, bf16)]
        outs.append(pltpu.VMEM(matrix.shape, bf16))
        scratch = []
    else:
        outs = [jax.ShapeDtypeStruct((own, voxels), f32 if k == 0 else bf16) for k in range(groups)]
        scratch = [pltpu.VMEM((groups * own, voxels), f32), pltpu.VMEM(matrix.shape, bf16)]
    return pl.pallas_call(
        kernel,
        out_shape=outs,
        in_specs=[SMEM, VMEM, HBM],
        out_specs=[VMEM] * len(outs),
        scratch_shapes=scratch + [pltpu.SemaphoreType.DMA((views * SPLIT,))],
        compiler_params=params(16),
        name="back_project",
    )(me, onchip(misfit), offchip(matrix))


def spread_misfit(half, other, sino, weight, copies):
    def kernel(half_ref, other_ref, sino_ref, weight_ref, out_ref):
        value = (weight_ref[...] * ((half_ref[...] + other_ref[...]) - sino_ref[...])).astype(bf16)
        for i in range(copies):
            out_ref[i] = value

    return pl.pallas_call(
        kernel,
        out_shape=jax.ShapeDtypeStruct((copies,) + half.shape, bf16),
        in_specs=[VMEM] * 4,
        out_specs=VMEM,
        compiler_params=params(4),
        name="spread_misfit",
    )(*[onchip(v) for v in (half, other, sino, weight)])


def halves(value):
    high = value.astype(bf16)
    return high, (value - high.astype(f32)).astype(bf16)


def product(weights, state_hi, state_lo):
    hi, lo = weights
    rows = hi.shape[0]
    both = jnp.dot(jnp.concatenate([hi, lo], axis=0), state_hi, preferred_element_type=f32)
    return both[:rows] + both[rows:] + jnp.dot(hi, state_lo, preferred_element_type=f32)


def denoise(low, own, high, first_in, middle, last_out, at, count):
    rows, width = own.shape
    depth, taps, hidden, _ = middle.shape
    step = taps * hidden // 3
    most = rows + 2 * (HALO - 1)
    tall = most + 2 + (-(most + 2)) % 8

    def kernel(at_ref, low_ref, own_ref, high_ref, first_ref, mid_ref, last_ref, out_ref, hi_ref, lo_ref):
        lane = lax.broadcasted_iota(jnp.int32, (1, LANES), 1)
        not_first = (lane != 0).astype(f32)
        not_last = (lane != LANES - 1).astype(f32)

        def shifted(value):
            left, right = [], []
            for b in range(width // LANES):
                piece = value[:, b * LANES : (b + 1) * LANES]
                left.append(pltpu.roll(piece, 1, 1) * not_first)
                right.append(pltpu.roll(piece, LANES - 1, 1) * not_last)
            return jnp.concatenate(left, axis=1), value, jnp.concatenate(right, axis=1)

        def keep(layer, row, values):
            reach = HALO - 1 - layer
            index = at_ref[0] * rows + (row - reach)
            inside = (index >= 0) & (index < count * rows)
            state = jnp.maximum(values, 0.0) * inside.astype(f32)
            for e, moved in enumerate(shifted(state)):
                at_row = step * row + hidden * e
                hi, lo = halves(moved)
                hi_ref[at_row : at_row + hidden, :] = hi
                lo_ref[at_row : at_row + hidden, :] = lo

        def banded(blocks, outs):
            blank = lambda n: [jnp.zeros((blocks[0].shape[0], n), f32)] if n else []
            return jnp.concatenate(
                [
                    jnp.concatenate(blank(step * i) + blocks + blank(step * (outs - 1 - i)), axis=1)
                    for i in range(outs)
                ],
                axis=0,
            )

        shape = (most, hidden, 3 * tall)
        out_row = lax.broadcasted_iota(jnp.int32, shape, 0)
        column = lax.broadcasted_iota(jnp.int32, shape, 2)
        spread = jnp.zeros(shape, f32)
        for tap in range(9):
            a, e = tap // 3, tap % 3
            chosen = column == out_row + (a + e * tall)
            spread = jnp.where(chosen, first_ref[:, tap : tap + 1][None], spread)
        spread = spread.reshape(most * hidden, 3 * tall)

        field = jnp.concatenate(
            [low_ref[...], own_ref[...], high_ref[...], jnp.zeros((tall - rows - 2 * HALO, width), f32)],
            axis=0,
        )
        state_hi, state_lo = halves(jnp.concatenate(shifted(field), axis=0))
        values = product(halves(spread), state_hi, state_lo)
        live = most
        for r in range(live):
            keep(0, r, values[hidden * r : hidden * (r + 1)])
        for layer in range(depth):
            weights = halves(banded([mid_ref[layer, t] for t in range(taps)], 3))
            live -= 2
            for r in range(0, live, 3):
                take = min(3, live - r)
                used = step * (take + 2)
                chunk = [w[: hidden * take, :used] for w in weights]
                state_hi = hi_ref[step * r : step * r + used, :]
                state_lo = lo_ref[step * r : step * r + used, :]
                values = product(chunk, state_hi, state_lo)
                for i in range(take):
                    keep(layer + 1, r + i, values[hidden * i : hidden * (i + 1)])
        used = step * live
        weights = halves(banded([last_ref[t : t + 1, :] for t in range(taps)], rows))
        out_ref[...] = own_ref[...] - product(weights, hi_ref[:used, :], lo_ref[:used, :])

    return pl.pallas_call(
        kernel,
        out_shape=jax.ShapeDtypeStruct((rows, width), f32),
        in_specs=[SMEM] + [VMEM] * 6,
        out_specs=VMEM,
        scratch_shapes=[pltpu.VMEM((most * step, width), bf16)] * 2,
        compiler_params=params(24),
        name="denoise",
    )(at, *[onchip(v) for v in (low, own, high, first_in, middle, last_out)])


def line(count, shift):
    return [(i, i + shift) for i in range(count) if 0 <= i + shift < count]


def from_below(field, axis, count):
    return lax.ppermute(field[-HALO:], axis, line(count, 1))


def from_above(field, axis, count):
    return lax.ppermute(field[:HALO], axis, line(count, -1))


def swap(value, agents, k):
    return lax.ppermute(value, "agent", [(i, i ^ k) for i in range(agents)])


def by_row(state):
    own, voxels = state.shape
    return state.reshape(own, PX, voxels // PX).transpose(1, 0, 2).reshape(PX, own * (voxels // PX))


def body(
    view_tile,
    block_mask,
    sinogram,
    bin_weight,
    model_state,
    planar_state,
    sagittal_state,
    planar_in,
    planar_mid,
    planar_out,
    sagittal_in,
    sagittal_mid,
    sagittal_out,
):
    agents = lax.axis_size("agent")
    tiles = lax.axis_size(TILE)
    spread = lax.axis_size(PLANE)
    spot = lax.axis_index(PLANE)
    own = model_state.shape[1]
    views, _, bins, _ = view_tile.shape
    per = views * agents * (bins // LANES) // spread
    agent = lax.axis_index("agent").reshape(1).astype(jnp.int32)
    tile_at = lax.axis_index(TILE).reshape(1).astype(jnp.int32)
    model_state, planar_state, sagittal_state = model_state[0], planar_state[0], sagittal_state[0]

    def share(values):
        tiled = values.reshape(views, agents, own, bins // LANES, LANES).transpose(0, 1, 3, 2, 4)
        return lax.dynamic_index_in_dim(tiled.reshape(spread, per, own, LANES), spot, 0, keepdims=False)

    def gathered(sent):
        got = lax.all_to_all(sent.reshape(spread, per, own, LANES), PLANE, 0, 0)
        half = got.astype(f32).sum(axis=0)
        other = lax.ppermute(half, "zh", [(0, 1), (1, 0)])
        spreaded = spread_misfit(half, other, share(sinogram), share(bin_weight), spread)
        misfit = lax.all_to_all(spreaded, PLANE, 0, 0)
        return misfit.reshape(spread * per, own, LANES)

    low = model_state.astype(bf16)
    parts = [low] + [swap(low, agents, k) for k in range(1, agents)]
    chip = mask_blocks(view_tile, block_mask)
    sent, anchor, matrix = project_first(parts, chip, agent)

    plane, plane_in, side_in, tile_at = lax.optimization_barrier(
        (by_row(planar_state), planar_in.T, sagittal_in.T, tile_at)
    )
    plane_low = from_below(plane, TILE, tiles)
    plane_high = from_above(plane, TILE, tiles)
    side_low = from_below(sagittal_state, "agent", agents)
    side_high = from_above(sagittal_state, "agent", agents)

    misfit = gathered(sent)
    total, piece, chip = back_project(misfit, matrix, agent, agents, True)
    pieces = [total] + [swap(piece, agents, k) for k in range(1, agents)]
    sent, gradient = project_next(anchor, pieces, chip, agent)
    guess = model_state - 0.5 * gradient

    misfit = gathered(sent)
    pieces = back_project(misfit, matrix, agent, agents, False)
    pieces = [pieces[0]] + [swap(pieces[k], agents, k) for k in range(1, agents)]
    gradient = sum(piece.astype(f32) for piece in pieces)
    model_image = guess - 0.5 * (gradient + (guess - model_state))

    planar_image = by_row(denoise(plane_low, plane, plane_high, plane_in, planar_mid, planar_out, tile_at, tiles))
    sagittal_image = denoise(side_low, sagittal_state, side_high, side_in, sagittal_mid, sagittal_out, agent, agents)

    reflect_model = 2.0 * model_image - model_state
    reflect_plane = 2.0 * planar_image - planar_state
    reflect_side = 2.0 * sagittal_image - sagittal_state
    consensus = 0.5 * reflect_model + 0.25 * reflect_plane + 0.25 * reflect_side
    model_next = 0.5 * model_state + 0.5 * (2.0 * consensus - reflect_model)
    planar_next = 0.5 * planar_state + 0.5 * (2.0 * consensus - reflect_plane)
    sagittal_next = 0.5 * sagittal_state + 0.5 * (2.0 * consensus - reflect_side)
    return (model_next[None], planar_next[None], sagittal_next[None])


def solution(mesh):
    fine = Mesh(mesh.devices.reshape(2, 4, 4, 2, 4), TILE + ("agent",))
    return jax.shard_map(
        body,
        mesh=fine,
        in_specs=(
            P("agent", TILE, None, None),
            P("agent", TILE, None, None),
            P("agent", None, None),
            P("agent", None, None),
            P(TILE, "agent", None),
            P(TILE, "agent", None),
            P(TILE, "agent", None),
            P(),
            P(),
            P(),
            P(),
            P(),
            P(),
        ),
        out_specs=(P(TILE, "agent", None),) * 3,
        check_vma=False,
    )
```

```python
import jax
import jax.numpy as jnp
from jax import lax
from jax.experimental import pallas as pl
from jax.experimental.pallas import tpu as pltpu
from jax.sharding import Mesh, PartitionSpec as P


PX = 8
HALO = 5
LANES = 128
SPLIT = 2
PLANE = ("x", "y", "core")
TILE = ("zh",) + PLANE

bf16 = jnp.bfloat16
f32 = jnp.float32
VMEM = pl.BlockSpec(memory_space=pltpu.VMEM)
SMEM = pl.BlockSpec(memory_space=pltpu.SMEM)
HBM = pl.BlockSpec(memory_space=pltpu.HBM)


def params(mebibytes, axes=0):
    return pltpu.CompilerParams(
        vmem_limit_bytes=mebibytes << 20, dimension_semantics=("arbitrary",) * axes or None
    )


def onchip(value):
    return pltpu.with_memory_space_constraint(value, pltpu.VMEM)


def fetch(source, target, sems):
    views, bins, _ = target.shape
    rows = bins // SPLIT
    copies = []
    for v in range(views):
        for h in range(SPLIT):
            copy = pltpu.make_async_copy(
                source.at[v, pl.ds(h * rows, rows)],
                target.at[v, pl.ds(h * rows, rows)],
                sems.at[v * SPLIT + h],
            )
            copy.start()
            copies.append((v, h * rows, copy))
    return copies


def offchip(value):
    return pltpu.with_memory_space_constraint(value, pltpu.HBM)


def mask_blocks(view_tile, mask):
    views, _, bins, voxels = view_tile.shape
    rows = bins // SPLIT

    def kernel(mask_ref, view_ref, chip_ref, sems):
        for v, first, copy in fetch(view_ref.at[:, 0], chip_ref, sems):
            copy.wait()
            for j in range(first, first + rows, LANES):
                for k in range(voxels // LANES):
                    keep = jnp.full((16, LANES), mask_ref[v, 0, j // LANES, k].astype(f32)).astype(bf16)
                    at = (v, slice(j, j + LANES), slice(k * LANES, (k + 1) * LANES))
                    block = chip_ref[at].reshape(8, 16, LANES) * keep[None]
                    chip_ref[at] = block.reshape(LANES, LANES)

    return pl.pallas_call(
        kernel,
        out_shape=pltpu.VMEM((views, bins, voxels), bf16),
        in_specs=[SMEM, HBM],
        out_specs=VMEM,
        scratch_shapes=[pltpu.SemaphoreType.DMA((views * SPLIT,))],
        compiler_params=params(16),
        name="mask_blocks",
    )(mask, offchip(view_tile))


def project_tiles(low, matrix_ref, out_ref):
    views, bins, _ = matrix_ref.shape
    groups, blocks = low.shape[0] // 8, bins // LANES
    for v in range(views):
        result = lax.dot_general(
            low, matrix_ref[v], (((1,), (1,)), ((), ())), preferred_element_type=f32
        ).astype(bf16)
        for g in range(groups):
            for j in range(blocks):
                out_ref[(v * groups + g) * blocks + j] = result[8 * g : 8 * g + 8, j * LANES : (j + 1) * LANES]


def project_first(parts, matrix, me):
    own, voxels = parts[0].shape
    groups = len(parts)
    views, bins, _ = matrix.shape

    def kernel(me_ref, *refs):
        part_refs, (matrix_ref, out_ref, anchor_ref, main_ref, sems) = refs[:groups], refs[groups:]
        copies = fetch(matrix_ref, main_ref, sems)
        for k in range(groups):
            first = pl.multiple_of(jnp.bitwise_xor(me_ref[0], k) * own, own)
            anchor_ref[pl.ds(first, own), :] = part_refs[k][...].astype(f32)
        project_tiles(anchor_ref[...].astype(bf16), matrix_ref, out_ref)
        for *_, copy in copies:
            copy.wait()

    return pl.pallas_call(
        kernel,
        out_shape=[
            jax.ShapeDtypeStruct((views * groups * bins // LANES, own, LANES), bf16),
            jax.ShapeDtypeStruct((groups * own, voxels), f32),
            pltpu.HBM(matrix.shape, bf16),
        ],
        in_specs=[SMEM] + [VMEM] * (groups + 1),
        out_specs=[VMEM, VMEM, HBM],
        scratch_shapes=[pltpu.SemaphoreType.DMA((views * SPLIT,))],
        compiler_params=params(16),
        name="project_first",
    )(me, *[onchip(p) for p in parts], onchip(matrix))


def project_next(anchor, pieces, matrix, me):
    slices, voxels = anchor.shape
    views, bins, _ = matrix.shape
    own = 8
    count = len(pieces)

    def kernel(me_ref, anchor_ref, *refs):
        piece_refs, (matrix_ref, out_ref, own_ref, gradient_ref) = refs[:count], refs[count:]
        gradient = piece_refs[0][...]
        for ref in piece_refs[1:]:
            gradient = gradient + ref[...].astype(f32)
        gradient_ref[...] = gradient
        low = (anchor_ref[...] - 0.5 * gradient).astype(bf16)
        own_ref[...] = gradient_ref[pl.ds(pl.multiple_of(me_ref[0] * own, own), own), :]
        project_tiles(low, matrix_ref, out_ref)

    return pl.pallas_call(
        kernel,
        out_shape=[
            jax.ShapeDtypeStruct((views * slices // own * bins // LANES, own, LANES), bf16),
            jax.ShapeDtypeStruct((own, voxels), f32),
        ],
        in_specs=[SMEM] + [VMEM] * (count + 2),
        out_specs=[VMEM, VMEM],
        scratch_shapes=[pltpu.VMEM((slices, voxels), f32)],
        compiler_params=params(16),
        name="project_next",
    )(me, onchip(anchor), *[onchip(p) for p in pieces], onchip(matrix))


def back_project(misfit, matrix, me, groups, whole):
    views, bins, voxels = matrix.shape
    own = misfit.shape[1]
    blocks = bins // LANES
    rows = bins // SPLIT

    def kernel(me_ref, misfit_ref, matrix_ref, *refs):
        *outs, chip_ref, sems = refs if whole else refs[:-3] + refs[-2:]
        total = None
        for v, first, copy in fetch(matrix_ref, chip_ref, sems):
            left = jnp.concatenate(
                [
                    jnp.concatenate(
                        [
                            misfit_ref[(v * groups + g) * blocks + j].astype(f32)
                            for j in range(first // LANES, (first + rows) // LANES)
                        ],
                        axis=1,
                    )
                    for g in range(groups)
                ],
                axis=0,
            ).astype(bf16)
            copy.wait()
            part = jnp.dot(left, chip_ref[v, first : first + rows, :], preferred_element_type=f32)
            total = part if total is None else total + part
        if whole:
            outs[0][...] = total
            outs[1][...] = total.astype(bf16)
        else:
            total_ref = refs[-3]
            total_ref[...] = total
            for k in range(groups):
                first = pl.multiple_of(jnp.bitwise_xor(me_ref[0], k) * own, own)
                outs[k][...] = total_ref[pl.ds(first, own), :].astype(outs[k].dtype)

    if whole:
        outs = [jax.ShapeDtypeStruct((groups * own, voxels), t) for t in (f32, bf16)]
        outs.append(pltpu.VMEM(matrix.shape, bf16))
        scratch = []
    else:
        outs = [jax.ShapeDtypeStruct((own, voxels), f32 if k == 0 else bf16) for k in range(groups)]
        scratch = [pltpu.VMEM((groups * own, voxels), f32), pltpu.VMEM(matrix.shape, bf16)]
    return pl.pallas_call(
        kernel,
        out_shape=outs,
        in_specs=[SMEM, VMEM, HBM],
        out_specs=[VMEM] * len(outs),
        scratch_shapes=scratch + [pltpu.SemaphoreType.DMA((views * SPLIT,))],
        compiler_params=params(16),
        name="back_project",
    )(me, onchip(misfit), offchip(matrix))


def spread_misfit(half, other, sino, weight, copies):
    def kernel(half_ref, other_ref, sino_ref, weight_ref, out_ref):
        value = (weight_ref[...] * ((half_ref[...] + other_ref[...]) - sino_ref[...])).astype(bf16)
        for i in range(copies):
            out_ref[i] = value

    return pl.pallas_call(
        kernel,
        out_shape=jax.ShapeDtypeStruct((copies,) + half.shape, bf16),
        in_specs=[VMEM] * 4,
        out_specs=VMEM,
        compiler_params=params(4),
        name="spread_misfit",
    )(*[onchip(v) for v in (half, other, sino, weight)])


def halves(value):
    high = value.astype(bf16)
    return high, (value - high.astype(f32)).astype(bf16)


def product(weights, state_hi, state_lo):
    hi, lo = weights
    rows = hi.shape[0]
    both = jnp.dot(jnp.concatenate([hi, lo], axis=0), state_hi, preferred_element_type=f32)
    return both[:rows] + both[rows:] + jnp.dot(hi, state_lo, preferred_element_type=f32)


def denoise(low, own, high, first_in, middle, last_out, at, count, across):
    rows, width = PX, own.shape[1]
    depth, taps, hidden, _ = middle.shape
    step = taps * hidden // 3
    most = rows + 2 * (HALO - 1)
    tall = most + 2 + (-(most + 2)) % 8

    def kernel(at_ref, low_ref, own_ref, high_ref, first_ref, mid_ref, last_ref, out_ref, hi_ref, lo_ref):
        lane = lax.broadcasted_iota(jnp.int32, (1, LANES), 1)
        not_first = (lane != 0).astype(f32)
        not_last = (lane != LANES - 1).astype(f32)

        def shifted(value):
            left, right = [], []
            for b in range(width // LANES):
                piece = value[:, b * LANES : (b + 1) * LANES]
                left.append(pltpu.roll(piece, 1, 1) * not_first)
                right.append(pltpu.roll(piece, LANES - 1, 1) * not_last)
            return jnp.concatenate(left, axis=1), value, jnp.concatenate(right, axis=1)

        def keep(layer, row, values):
            reach = HALO - 1 - layer
            index = at_ref[0] * rows + (row - reach)
            inside = (index >= 0) & (index < count * rows)
            state = jnp.maximum(values, 0.0) * inside.astype(f32)
            for e, moved in enumerate(shifted(state)):
                at_row = step * row + hidden * e
                hi, lo = halves(moved)
                hi_ref[at_row : at_row + hidden, :] = hi
                lo_ref[at_row : at_row + hidden, :] = lo

        def banded(blocks, outs):
            blank = lambda n: [jnp.zeros((blocks[0].shape[0], n), f32)] if n else []
            return jnp.concatenate(
                [
                    jnp.concatenate(blank(step * i) + blocks + blank(step * (outs - 1 - i)), axis=1)
                    for i in range(outs)
                ],
                axis=0,
            )

        def turned(tiles):
            turn = jnp.swapaxes(jnp.stack(tiles), 0, 1)
            return jnp.concatenate([turn[b] for b in range(turn.shape[0])], axis=1)

        def cut(value):
            return [value[:, i : i + LANES] for i in range(0, value.shape[1], LANES)]

        spare = tall - rows - 2 * HALO
        if across:
            tiles = cut(low_ref[...]) + cut(own_ref[...]) + cut(high_ref[...])
            field = turned(tiles + [jnp.zeros_like(tiles[0])] * spare)
        else:
            field = jnp.concatenate(
                [low_ref[...], own_ref[...], high_ref[...], jnp.zeros((spare, width), f32)], axis=0
            )

        square = jnp.concatenate([first_ref[...], jnp.zeros((taps, LANES - hidden), f32)], axis=1)
        square = jnp.concatenate([square, jnp.zeros((LANES - taps, LANES), f32)], axis=0)
        first_taps = square.T[:hidden]
        shape = (most, hidden, 3 * tall)
        out_row = lax.broadcasted_iota(jnp.int32, shape, 0)
        column = lax.broadcasted_iota(jnp.int32, shape, 2)
        spread = jnp.zeros(shape, f32)
        for tap in range(9):
            a, e = tap // 3, tap % 3
            chosen = column == out_row + (a + e * tall)
            spread = jnp.where(chosen, first_taps[:, tap : tap + 1][None], spread)
        spread = spread.reshape(most * hidden, 3 * tall)

        state_hi, state_lo = halves(jnp.concatenate(shifted(field), axis=0))
        values = product(halves(spread), state_hi, state_lo)
        live = most
        for r in range(live):
            keep(0, r, values[hidden * r : hidden * (r + 1)])
        for layer in range(depth):
            weights = halves(banded([mid_ref[layer, t] for t in range(taps)], 3))
            live -= 2
            for r in range(0, live, 3):
                take = min(3, live - r)
                used = step * (take + 2)
                chunk = [w[: hidden * take, :used] for w in weights]
                state_hi = hi_ref[step * r : step * r + used, :]
                state_lo = lo_ref[step * r : step * r + used, :]
                values = product(chunk, state_hi, state_lo)
                for i in range(take):
                    keep(layer + 1, r + i, values[hidden * i : hidden * (i + 1)])
        used = step * live
        weights = halves(banded([last_ref[t : t + 1, :] for t in range(taps)], rows))
        change = product(weights, hi_ref[:used, :], lo_ref[:used, :])
        out_ref[...] = own_ref[...] - (turned(cut(change)) if across else change)

    return pl.pallas_call(
        kernel,
        out_shape=jax.ShapeDtypeStruct((rows, width), f32),
        in_specs=[SMEM] + [VMEM] * 6,
        out_specs=VMEM,
        scratch_shapes=[pltpu.VMEM((most * step, width), bf16)] * 2,
        compiler_params=params(24),
        name="denoise",
    )(at, *[onchip(v) for v in (low, own, high, first_in, middle, last_out)])


def line(count, shift):
    return [(i, i + shift) for i in range(count) if 0 <= i + shift < count]


def swap(value, agents, k):
    return lax.ppermute(value, "agent", [(i, i ^ k) for i in range(agents)])


def join(model_state, planar_state, sagittal_state, gradient, pieces, planar_image, sagittal_image):
    count = len(pieces)

    def kernel(*refs):
        model, plane, side, first, plane_image, side_image = [r[...] for r in refs[:6]]
        piece_refs, outs = refs[6 : 6 + count], refs[6 + count :]
        second = piece_refs[0][...]
        for ref in piece_refs[1:]:
            second = second + ref[...].astype(f32)
        guess = model - 0.5 * first
        model_image = guess - 0.5 * (second + (guess - model))
        reflect_model = 2.0 * model_image - model
        reflect_plane = 2.0 * plane_image - plane
        reflect_side = 2.0 * side_image - side
        consensus = 0.5 * reflect_model + 0.25 * reflect_plane + 0.25 * reflect_side
        outs[0][0] = 0.5 * model + 0.5 * (2.0 * consensus - reflect_model)
        outs[1][0] = 0.5 * plane + 0.5 * (2.0 * consensus - reflect_plane)
        outs[2][0] = 0.5 * side + 0.5 * (2.0 * consensus - reflect_side)

    values = (model_state, planar_state, sagittal_state, gradient, planar_image, sagittal_image, *pieces)
    return pl.pallas_call(
        kernel,
        out_shape=[jax.ShapeDtypeStruct((1,) + model_state.shape, f32)] * 3,
        in_specs=[VMEM] * len(values),
        out_specs=[VMEM] * 3,
        compiler_params=params(4),
        name="join",
    )(*[onchip(v) for v in values])


def body(
    view_tile,
    block_mask,
    sinogram,
    bin_weight,
    model_state,
    planar_state,
    sagittal_state,
    planar_in,
    planar_mid,
    planar_out,
    sagittal_in,
    sagittal_mid,
    sagittal_out,
):
    agents = lax.axis_size("agent")
    tiles = lax.axis_size(TILE)
    spread = lax.axis_size(PLANE)
    spot = lax.axis_index(PLANE)
    own = model_state.shape[1]
    views, _, bins, _ = view_tile.shape
    per = views * agents * (bins // LANES) // spread
    agent = lax.axis_index("agent").reshape(1).astype(jnp.int32)
    tile_at = lax.axis_index(TILE).reshape(1).astype(jnp.int32)
    model_state, planar_state, sagittal_state = model_state[0], planar_state[0], sagittal_state[0]

    def share(values):
        tiled = values.reshape(views, agents, own, bins // LANES, LANES).transpose(0, 1, 3, 2, 4)
        return lax.dynamic_index_in_dim(tiled.reshape(spread, per, own, LANES), spot, 0, keepdims=False)

    def gathered(sent):
        got = lax.all_to_all(sent.reshape(spread, per, own, LANES), PLANE, 0, 0)
        half = got.astype(f32).sum(axis=0)
        other = lax.ppermute(half, "zh", [(0, 1), (1, 0)])
        spreaded = spread_misfit(half, other, share(sinogram), share(bin_weight), spread)
        misfit = lax.all_to_all(spreaded, PLANE, 0, 0)
        return misfit.reshape(spread * per, own, LANES)

    low = model_state.astype(bf16)
    parts = [low] + [swap(low, agents, k) for k in range(1, agents)]
    chip = mask_blocks(view_tile, block_mask)
    sent, anchor, matrix = project_first(parts, chip, agent)

    edge = HALO * LANES
    sent, plane, side, tile_at = lax.optimization_barrier((sent, planar_state, sagittal_state, tile_at))
    plane_low = lax.ppermute(plane[:, -edge:], TILE, line(tiles, 1))
    plane_high = lax.ppermute(plane[:, :edge], TILE, line(tiles, -1))
    side_low = lax.ppermute(side[-HALO:], "agent", line(agents, 1))
    side_high = lax.ppermute(side[:HALO], "agent", line(agents, -1))

    misfit = gathered(sent)
    total, piece, chip = back_project(misfit, matrix, agent, agents, True)
    pieces = [total] + [swap(piece, agents, k) for k in range(1, agents)]
    sent, gradient = project_next(anchor, pieces, chip, agent)
    misfit = gathered(sent)
    pieces = back_project(misfit, matrix, agent, agents, False)
    pieces = [pieces[0]] + [swap(pieces[k], agents, k) for k in range(1, agents)]
    kernels = (planar_in, planar_mid, planar_out)
    planar_image = denoise(plane_low, planar_state, plane_high, *kernels, tile_at, tiles, True)
    kernels = (sagittal_in, sagittal_mid, sagittal_out)
    sagittal_image = denoise(side_low, sagittal_state, side_high, *kernels, agent, agents, False)
    states = (model_state, planar_state, sagittal_state)
    return join(*states, gradient, pieces, planar_image, sagittal_image)


def solution(mesh):
    fine = Mesh(mesh.devices.reshape(2, 4, 4, 2, 4), TILE + ("agent",))
    return jax.shard_map(
        body,
        mesh=fine,
        in_specs=(
            P("agent", TILE, None, None),
            P("agent", TILE, None, None),
            P("agent", None, None),
            P("agent", None, None),
            P(TILE, "agent", None),
            P(TILE, "agent", None),
            P(TILE, "agent", None),
            P(),
            P(),
            P(),
            P(),
            P(),
            P(),
        ),
        out_specs=(P(TILE, "agent", None),) * 3,
        check_vma=False,
    )
```

```python
import jax
import jax.numpy as jnp
from jax import lax
from jax.experimental import pallas as pl
from jax.experimental.pallas import tpu as pltpu
from jax.sharding import Mesh, PartitionSpec as P


PX = 8
HALO = 5
LANES = 128
SPLIT = 2
KEPT = 3
PLANE = ("x", "y", "core")
TILE = ("zh",) + PLANE

bf16 = jnp.bfloat16
f32 = jnp.float32
VMEM = pl.BlockSpec(memory_space=pltpu.VMEM)
SMEM = pl.BlockSpec(memory_space=pltpu.SMEM)
HBM = pl.BlockSpec(memory_space=pltpu.HBM)


def params(mebibytes, axes=0):
    return pltpu.CompilerParams(
        vmem_limit_bytes=mebibytes << 20, dimension_semantics=("arbitrary",) * axes or None
    )


def onchip(value):
    return pltpu.with_memory_space_constraint(value, pltpu.VMEM)


def fetch(source, target, sems):
    copies = []
    for i in range(target.shape[0]):
        copy = pltpu.make_async_copy(source.at[i], target.at[i], sems.at[i])
        copy.start()
        copies.append(copy)
    return copies


def offchip(value):
    return pltpu.with_memory_space_constraint(value, pltpu.HBM)


def mask_blocks(view_tile, mask):
    views, _, bins, voxels = view_tile.shape
    rows = bins // SPLIT
    pieces = views * SPLIT

    def kernel(mask_ref, view_ref, kept_ref, rest_ref, sems):
        places = [kept_ref.at[i] for i in range(KEPT)] + [rest_ref.at[i] for i in range(pieces - KEPT)]
        copies = []
        for i, place in enumerate(places):
            source = view_ref.at[i // SPLIT, 0, pl.ds(i % SPLIT * rows, rows)]
            copies.append(pltpu.make_async_copy(source, place, sems.at[i]))
            copies[-1].start()
        for i, place in enumerate(places):
            copies[i].wait()
            for j in range(rows // LANES):
                for k in range(voxels // LANES):
                    empty = mask_ref[i // SPLIT, i % SPLIT * (rows // LANES) + j, 0, k] == 0
                    at = (slice(j * LANES, (j + 1) * LANES), slice(k * LANES, (k + 1) * LANES))

                    @pl.when(empty)
                    def _(place=place, at=at):
                        place[at] = jnp.zeros((LANES, LANES), bf16)

    return pl.pallas_call(
        kernel,
        out_shape=[pltpu.VMEM((n, rows, voxels), bf16) for n in (KEPT, pieces - KEPT)],
        in_specs=[SMEM, HBM],
        out_specs=[VMEM, VMEM],
        scratch_shapes=[pltpu.SemaphoreType.DMA((pieces,))],
        compiler_params=params(16),
        name="mask_blocks",
    )(offchip(mask), offchip(view_tile))


def piece_list(*refs):
    return [(ref, i) for ref in refs for i in range(ref.shape[0])]


def project_tiles(low, pieces, out_ref):
    groups = low.shape[0] // 8
    for n, (ref, i) in enumerate(pieces):
        result = lax.dot_general(
            low, ref[i], (((1,), (1,)), ((), ())), preferred_element_type=f32
        ).astype(bf16)
        blocks = ref.shape[1] // LANES
        for g in range(groups):
            for j in range(blocks):
                at = (n // SPLIT * groups + g) * (SPLIT * blocks) + n % SPLIT * blocks + j
                out_ref[at] = result[8 * g : 8 * g + 8, j * LANES : (j + 1) * LANES]


def project_first(parts, kept, rest, me):
    own, voxels = parts[0].shape
    groups = len(parts)
    tiles = (kept.shape[0] + rest.shape[0]) * groups * kept.shape[1] // LANES

    def kernel(me_ref, *refs):
        part_refs, (kept_ref, rest_ref, out_ref, anchor_ref, main_ref, sems) = refs[:groups], refs[groups:]
        copies = fetch(rest_ref, main_ref, sems)
        for k in range(groups):
            first = pl.multiple_of(jnp.bitwise_xor(me_ref[0], k) * own, own)
            anchor_ref[pl.ds(first, own), :] = part_refs[k][...]
        project_tiles(anchor_ref[...].astype(bf16), piece_list(kept_ref, rest_ref), out_ref)
        for copy in copies:
            copy.wait()

    return pl.pallas_call(
        kernel,
        out_shape=[
            jax.ShapeDtypeStruct((tiles, own, LANES), bf16),
            jax.ShapeDtypeStruct((groups * own, voxels), f32),
            pltpu.HBM(rest.shape, bf16),
        ],
        in_specs=[SMEM] + [VMEM] * (groups + 2),
        out_specs=[VMEM, VMEM, HBM],
        scratch_shapes=[pltpu.SemaphoreType.DMA((rest.shape[0],))],
        compiler_params=params(16),
        name="project_first",
    )(me, *[onchip(p) for p in parts], onchip(kept), onchip(rest))


def project_next(anchor, pieces, kept, rest, me):
    slices, voxels = anchor.shape
    own = 8
    count = len(pieces)
    tiles = (kept.shape[0] + rest.shape[0]) * (slices // own) * kept.shape[1] // LANES

    def kernel(me_ref, anchor_ref, *refs):
        piece_refs, (kept_ref, rest_ref, out_ref, own_ref, gradient_ref) = refs[:count], refs[count:]
        gradient = piece_refs[0][...]
        for ref in piece_refs[1:]:
            gradient = gradient + ref[...].astype(f32)
        gradient_ref[...] = gradient
        low = (anchor_ref[...] - 0.5 * gradient).astype(bf16)
        own_ref[...] = gradient_ref[pl.ds(pl.multiple_of(me_ref[0] * own, own), own), :]
        project_tiles(low, piece_list(kept_ref, rest_ref), out_ref)

    return pl.pallas_call(
        kernel,
        out_shape=[
            jax.ShapeDtypeStruct((tiles, own, LANES), bf16),
            jax.ShapeDtypeStruct((own, voxels), f32),
        ],
        in_specs=[SMEM] + [VMEM] * (count + 3),
        out_specs=[VMEM, VMEM],
        scratch_shapes=[pltpu.VMEM((slices, voxels), f32)],
        compiler_params=params(16),
        name="project_next",
    )(me, onchip(anchor), *[onchip(p) for p in pieces], onchip(kept), onchip(rest))


def back_project(misfit, kept, main, me, groups, whole):
    rows, voxels = kept.shape[1:]
    own = misfit.shape[1]
    blocks = rows // LANES

    def kernel(me_ref, misfit_ref, kept_ref, main_ref, *refs):
        *outs, rest_ref, sems = refs if whole else refs[:-3] + refs[-2:]
        copies = [None] * KEPT + fetch(main_ref, rest_ref, sems)
        total = None
        for n, (ref, i) in enumerate(piece_list(kept_ref, rest_ref)):
            left = jnp.concatenate(
                [
                    jnp.concatenate(
                        [
                            misfit_ref[(n // SPLIT * groups + g) * (SPLIT * blocks) + n % SPLIT * blocks + j].astype(f32)
                            for j in range(blocks)
                        ],
                        axis=1,
                    )
                    for g in range(groups)
                ],
                axis=0,
            ).astype(bf16)
            if copies[n] is not None:
                copies[n].wait()
            part = jnp.dot(left, ref[i], preferred_element_type=f32)
            total = part if total is None else total + part
        if whole:
            outs[0][...] = total
            outs[1][...] = total.astype(bf16)
        else:
            total_ref = refs[-3]
            total_ref[...] = total
            for k in range(groups):
                first = pl.multiple_of(jnp.bitwise_xor(me_ref[0], k) * own, own)
                outs[k][...] = total_ref[pl.ds(first, own), :].astype(outs[k].dtype)

    if whole:
        outs = [jax.ShapeDtypeStruct((groups * own, voxels), t) for t in (f32, bf16)]
        outs.append(pltpu.VMEM(main.shape, bf16))
        scratch = []
    else:
        outs = [jax.ShapeDtypeStruct((own, voxels), f32 if k == 0 else bf16) for k in range(groups)]
        scratch = [pltpu.VMEM((groups * own, voxels), f32), pltpu.VMEM(main.shape, bf16)]
    return pl.pallas_call(
        kernel,
        out_shape=outs,
        in_specs=[SMEM, VMEM, VMEM, HBM],
        out_specs=[VMEM] * len(outs),
        scratch_shapes=scratch + [pltpu.SemaphoreType.DMA((main.shape[0],))],
        compiler_params=params(16),
        name="back_project",
    )(me, onchip(misfit), onchip(kept), offchip(main))


def spread_misfit(half, other, sino, weight, copies):
    def kernel(half_ref, other_ref, sino_ref, weight_ref, out_ref):
        value = (weight_ref[...] * ((half_ref[...] + other_ref[...]) - sino_ref[...])).astype(bf16)
        for i in range(copies):
            out_ref[i] = value

    return pl.pallas_call(
        kernel,
        out_shape=jax.ShapeDtypeStruct((copies,) + half.shape, bf16),
        in_specs=[VMEM] * 4,
        out_specs=VMEM,
        compiler_params=params(4),
        name="spread_misfit",
    )(*[onchip(v) for v in (half, other, sino, weight)])


def halves(value):
    high = value.astype(bf16)
    return high, (value - high.astype(f32)).astype(bf16)


def product(weights, state_hi, state_lo):
    hi, lo = weights
    rows = hi.shape[0]
    both = jnp.dot(jnp.concatenate([hi, lo], axis=0), state_hi, preferred_element_type=f32)
    return both[:rows] + both[rows:] + jnp.dot(hi, state_lo, preferred_element_type=f32)


def denoise(low, own, high, first_in, middle, last_out, at, count, across):
    rows, width = PX, own.shape[1]
    depth, taps, hidden, _ = middle.shape
    step = taps * hidden // 3
    most = rows + 2 * (HALO - 1)
    tall = most + 2 + (-(most + 2)) % 8

    def kernel(at_ref, low_ref, own_ref, high_ref, first_ref, mid_ref, last_ref, out_ref, hi_ref, lo_ref):
        lane = lax.broadcasted_iota(jnp.int32, (1, LANES), 1)
        not_first = (lane != 0).astype(f32)
        not_last = (lane != LANES - 1).astype(f32)

        def shifted(value):
            left, right = [], []
            for b in range(width // LANES):
                piece = value[:, b * LANES : (b + 1) * LANES]
                left.append(pltpu.roll(piece, 1, 1) * not_first)
                right.append(pltpu.roll(piece, LANES - 1, 1) * not_last)
            return jnp.concatenate(left, axis=1), value, jnp.concatenate(right, axis=1)

        def keep(layer, row, values):
            reach = HALO - 1 - layer
            index = at_ref[0] * rows + (row - reach)
            inside = (index >= 0) & (index < count * rows)
            state = jnp.maximum(values, 0.0) * inside.astype(f32)
            for e, moved in enumerate(shifted(state)):
                at_row = step * row + hidden * e
                hi, lo = halves(moved)
                hi_ref[at_row : at_row + hidden, :] = hi
                lo_ref[at_row : at_row + hidden, :] = lo

        def banded(blocks, outs):
            blank = lambda n: [jnp.zeros((blocks[0].shape[0], n), f32)] if n else []
            return jnp.concatenate(
                [
                    jnp.concatenate(blank(step * i) + blocks + blank(step * (outs - 1 - i)), axis=1)
                    for i in range(outs)
                ],
                axis=0,
            )

        def turned(tiles):
            turn = jnp.swapaxes(jnp.stack(tiles), 0, 1)
            return jnp.concatenate([turn[b] for b in range(turn.shape[0])], axis=1)

        def cut(value):
            return [value[:, i : i + LANES] for i in range(0, value.shape[1], LANES)]

        spare = tall - rows - 2 * HALO
        if across:
            tiles = cut(low_ref[...]) + cut(own_ref[...]) + cut(high_ref[...])
            field = turned(tiles + [jnp.zeros_like(tiles[0])] * spare)
        else:
            field = jnp.concatenate(
                [low_ref[...], own_ref[...], high_ref[...], jnp.zeros((spare, width), f32)], axis=0
            )

        square = jnp.concatenate([first_ref[...], jnp.zeros((taps, LANES - hidden), f32)], axis=1)
        square = jnp.concatenate([square, jnp.zeros((LANES - taps, LANES), f32)], axis=0)
        first_taps = square.T[:hidden]
        shape = (most, hidden, 3 * tall)
        out_row = lax.broadcasted_iota(jnp.int32, shape, 0)
        column = lax.broadcasted_iota(jnp.int32, shape, 2)
        spread = jnp.zeros(shape, f32)
        for tap in range(9):
            a, e = tap // 3, tap % 3
            chosen = column == out_row + (a + e * tall)
            spread = jnp.where(chosen, first_taps[:, tap : tap + 1][None], spread)
        spread = spread.reshape(most * hidden, 3 * tall)

        state_hi, state_lo = halves(jnp.concatenate(shifted(field), axis=0))
        values = product(halves(spread), state_hi, state_lo)
        live = most
        for r in range(live):
            keep(0, r, values[hidden * r : hidden * (r + 1)])
        for layer in range(depth):
            weights = halves(banded([mid_ref[layer, t] for t in range(taps)], 3))
            live -= 2
            for r in range(0, live, 3):
                take = min(3, live - r)
                used = step * (take + 2)
                chunk = [w[: hidden * take, :used] for w in weights]
                state_hi = hi_ref[step * r : step * r + used, :]
                state_lo = lo_ref[step * r : step * r + used, :]
                values = product(chunk, state_hi, state_lo)
                for i in range(take):
                    keep(layer + 1, r + i, values[hidden * i : hidden * (i + 1)])
        used = step * live
        weights = halves(banded([last_ref[t : t + 1, :] for t in range(taps)], rows))
        change = product(weights, hi_ref[:used, :], lo_ref[:used, :])
        out_ref[...] = own_ref[...] - (turned(cut(change)) if across else change)

    return pl.pallas_call(
        kernel,
        out_shape=jax.ShapeDtypeStruct((rows, width), f32),
        in_specs=[SMEM] + [VMEM] * 6,
        out_specs=VMEM,
        scratch_shapes=[pltpu.VMEM((most * step, width), bf16)] * 2,
        compiler_params=params(24),
        name="denoise",
    )(at, *[onchip(v) for v in (low, own, high, first_in, middle, last_out)])


def line(count, shift):
    return [(i, i + shift) for i in range(count) if 0 <= i + shift < count]


def swap(value, count, k, axis="agent"):
    return lax.ppermute(value, axis, [(i, i ^ k) for i in range(count)])


def join(model_state, planar_state, sagittal_state, gradient, pieces, planar_image, sagittal_image):
    count = len(pieces)

    def kernel(*refs):
        model, plane, side, first, plane_image, side_image = [r[...] for r in refs[:6]]
        piece_refs, outs = refs[6 : 6 + count], refs[6 + count :]
        second = piece_refs[0][...]
        for ref in piece_refs[1:]:
            second = second + ref[...].astype(f32)
        guess = model - 0.5 * first
        model_image = guess - 0.5 * (second + (guess - model))
        reflect_model = 2.0 * model_image - model
        reflect_plane = 2.0 * plane_image - plane
        reflect_side = 2.0 * side_image - side
        consensus = 0.5 * reflect_model + 0.25 * reflect_plane + 0.25 * reflect_side
        outs[0][0] = 0.5 * model + 0.5 * (2.0 * consensus - reflect_model)
        outs[1][0] = 0.5 * plane + 0.5 * (2.0 * consensus - reflect_plane)
        outs[2][0] = 0.5 * side + 0.5 * (2.0 * consensus - reflect_side)

    values = (model_state, planar_state, sagittal_state, gradient, planar_image, sagittal_image, *pieces)
    return pl.pallas_call(
        kernel,
        out_shape=[jax.ShapeDtypeStruct((1,) + model_state.shape, f32)] * 3,
        in_specs=[VMEM] * len(values),
        out_specs=[VMEM] * 3,
        compiler_params=params(4),
        name="join",
    )(*[onchip(v) for v in values])


def body(
    view_tile,
    block_mask,
    sinogram,
    bin_weight,
    model_state,
    planar_state,
    sagittal_state,
    planar_in,
    planar_mid,
    planar_out,
    sagittal_in,
    sagittal_mid,
    sagittal_out,
):
    agents = lax.axis_size("agent")
    tiles = lax.axis_size(TILE)
    spread = lax.axis_size(PLANE)
    spot = lax.axis_index(PLANE)
    own = model_state.shape[1]
    views, _, bins, _ = view_tile.shape
    per = views * agents * (bins // LANES) // spread
    agent = lax.axis_index("agent").reshape(1).astype(jnp.int32)
    tile_at = lax.axis_index(TILE).reshape(1).astype(jnp.int32)
    model_state, planar_state, sagittal_state = model_state[0], planar_state[0], sagittal_state[0]

    def share(values):
        tiled = values.reshape(views, agents, own, bins // LANES, LANES).transpose(0, 1, 3, 2, 4)
        return lax.dynamic_index_in_dim(tiled.reshape(spread, per, own, LANES), spot, 0, keepdims=False)

    def gathered(sent, sinogram, bin_weight):
        got = lax.all_to_all(sent.reshape(spread, per, own, LANES), PLANE, 0, 0)
        half = got.astype(f32).sum(axis=0)
        other = lax.ppermute(half, "zh", [(0, 1), (1, 0)])
        spreaded = spread_misfit(half, other, share(sinogram), share(bin_weight), spread)
        misfit = lax.all_to_all(spreaded, PLANE, 0, 0)
        return misfit.reshape(spread * per, own, LANES)

    parts = [model_state] + [swap(model_state, agents, k) for k in range(1, agents)]
    kept, rest = mask_blocks(view_tile, block_mask.transpose(0, 2, 1, 3))
    sent, anchor, main = project_first(parts, kept, rest, agent)

    edge = HALO * LANES
    sent, plane, side, tile_at, sinogram, bin_weight = lax.optimization_barrier(
        (sent, planar_state, sagittal_state, tile_at, sinogram, bin_weight)
    )
    begin, end = plane[:, :edge], plane[:, -edge:]
    ends = spot == spread - 1
    across = swap(jnp.where(ends, end, begin), 2, 1, "zh")
    upper = lax.axis_index("zh") == 1
    blank = jnp.zeros_like(begin)
    up = jnp.where(ends, jnp.where(upper, across, blank), end)
    down = jnp.where(spot == 0, jnp.where(upper, blank, across), begin)
    plane_low = lax.ppermute(up, PLANE, [(i, (i + 1) % spread) for i in range(spread)])
    plane_high = lax.ppermute(down, PLANE, [((i + 1) % spread, i) for i in range(spread)])
    side_low = lax.ppermute(side[-HALO:], "agent", line(agents, 1))
    side_high = lax.ppermute(side[:HALO], "agent", line(agents, -1))

    misfit = gathered(sent, sinogram, bin_weight)
    total, piece, rest = back_project(misfit, kept, main, agent, agents, True)
    pieces = [total] + [swap(piece, agents, k) for k in range(1, agents)]
    sent, gradient = project_next(anchor, pieces, kept, rest, agent)
    misfit = gathered(sent, sinogram, bin_weight)
    pieces = back_project(misfit, kept, main, agent, agents, False)
    pieces = [pieces[0]] + [swap(pieces[k], agents, k) for k in range(1, agents)]
    kernels = (planar_in, planar_mid, planar_out)
    planar_image = denoise(plane_low, planar_state, plane_high, *kernels, tile_at, tiles, True)
    kernels = (sagittal_in, sagittal_mid, sagittal_out)
    sagittal_image = denoise(side_low, sagittal_state, side_high, *kernels, agent, agents, False)
    states = (model_state, planar_state, sagittal_state)
    return join(*states, gradient, pieces, planar_image, sagittal_image)


def solution(mesh):
    fine = Mesh(mesh.devices.reshape(2, 4, 4, 2, 4), TILE + ("agent",))
    return jax.shard_map(
        body,
        mesh=fine,
        in_specs=(
            P("agent", TILE, None, None),
            P("agent", TILE, None, None),
            P("agent", None, None),
            P("agent", None, None),
            P(TILE, "agent", None),
            P(TILE, "agent", None),
            P(TILE, "agent", None),
            P(),
            P(),
            P(),
            P(),
            P(),
            P(),
        ),
        out_specs=(P(TILE, "agent", None),) * 3,
        check_vma=False,
    )
```

```python
import jax
import jax.numpy as jnp
from jax import lax
from jax.experimental import pallas as pl
from jax.experimental.pallas import tpu as pltpu
from jax.sharding import Mesh, PartitionSpec as P


PX = 8
HALO = 5
LANES = 128
SPLIT = 2
KEPT = 3
PLANE = ("x", "y", "core")
TILE = ("zh",) + PLANE

bf16 = jnp.bfloat16
f32 = jnp.float32
VMEM = pl.BlockSpec(memory_space=pltpu.VMEM)
HBM = pl.BlockSpec(memory_space=pltpu.HBM)


def params(mebibytes, axes=0):
    return pltpu.CompilerParams(
        vmem_limit_bytes=mebibytes << 20, dimension_semantics=("arbitrary",) * axes or None
    )


def onchip(value):
    return pltpu.with_memory_space_constraint(value, pltpu.VMEM)


def fetch(source, target, sems):
    copies = []
    for i in range(target.shape[0]):
        copy = pltpu.make_async_copy(source.at[i], target.at[i], sems.at[i])
        copy.start()
        copies.append(copy)
    return copies


def offchip(value):
    return pltpu.with_memory_space_constraint(value, pltpu.HBM)


def mask_blocks(view_tile, mask):
    views, _, bins, voxels = view_tile.shape
    rows = bins // SPLIT
    pieces = views * SPLIT

    def kernel(mask_main, view_ref, kept_ref, rest_ref, mask_ref, mask_sem, sems):
        mask_copy = pltpu.make_async_copy(mask_main, mask_ref, mask_sem)
        mask_copy.start()
        places = [kept_ref.at[i] for i in range(KEPT)] + [rest_ref.at[i] for i in range(pieces - KEPT)]
        copies = []
        for i, place in enumerate(places):
            source = view_ref.at[i // SPLIT, 0, pl.ds(i % SPLIT * rows, rows)]
            copies.append(pltpu.make_async_copy(source, place, sems.at[i]))
            copies[-1].start()
        mask_copy.wait()
        for i, place in enumerate(places):
            copies[i].wait()
            for j in range(rows // LANES):
                for k in range(voxels // LANES):
                    empty = mask_ref[i // SPLIT, i % SPLIT * (rows // LANES) + j, 0, k] == 0
                    at = (slice(j * LANES, (j + 1) * LANES), slice(k * LANES, (k + 1) * LANES))

                    @pl.when(empty)
                    def _(place=place, at=at):
                        place[at] = jnp.zeros((LANES, LANES), bf16)

    return pl.pallas_call(
        kernel,
        out_shape=[pltpu.VMEM((n, rows, voxels), bf16) for n in (KEPT, pieces - KEPT)],
        in_specs=[HBM, HBM],
        out_specs=[VMEM, VMEM],
        scratch_shapes=[
            pltpu.SMEM(mask.shape, mask.dtype),
            pltpu.SemaphoreType.DMA,
            pltpu.SemaphoreType.DMA((pieces,)),
        ],
        compiler_params=params(16),
        name="mask_blocks",
    )(offchip(mask), offchip(view_tile))


def piece_list(*refs):
    return [(ref, i) for ref in refs for i in range(ref.shape[0])]


def project_tiles(low, pieces, tile_ref, out_ref, sems):
    groups = low.shape[0] // 8
    copies = []
    for n, (ref, i) in enumerate(pieces):
        result = lax.dot_general(
            low, ref[i], (((1,), (1,)), ((), ())), preferred_element_type=f32
        ).astype(bf16)
        blocks = ref.shape[1] // LANES
        size = groups * SPLIT * blocks
        for g in range(groups):
            for j in range(blocks):
                at = n // SPLIT * size + g * SPLIT * blocks + n % SPLIT * blocks + j
                tile_ref[at] = result[8 * g : 8 * g + 8, j * LANES : (j + 1) * LANES]
        if n % SPLIT == SPLIT - 1:
            v = n // SPLIT
            span = pl.ds(v * size, size)
            copies.append(pltpu.make_async_copy(tile_ref.at[span], out_ref.at[span], sems.at[v]))
            copies[-1].start()
    return copies


def project_first(parts, kept, rest, me):
    own, voxels = parts[0].shape
    groups = len(parts)
    tiles = (kept.shape[0] + rest.shape[0]) * groups * kept.shape[1] // LANES

    def kernel(*refs):
        part_refs, rest_refs = refs[:groups], refs[groups:]
        kept_ref, rest_ref, out_ref, anchor_ref, main_ref, tile_ref, out_sems, sems = rest_refs
        copies = fetch(rest_ref, main_ref, sems)
        for k in range(groups):
            first = pl.multiple_of(jnp.bitwise_xor(me(), k) * own, own)
            anchor_ref[pl.ds(first, own), :] = part_refs[k][...]
        pieces = piece_list(kept_ref, rest_ref)
        copies += project_tiles(anchor_ref[...].astype(bf16), pieces, tile_ref, out_ref, out_sems)
        for copy in copies:
            copy.wait()

    return pl.pallas_call(
        kernel,
        out_shape=[
            pltpu.HBM((tiles, own, LANES), bf16),
            jax.ShapeDtypeStruct((groups * own, voxels), f32),
            pltpu.HBM(rest.shape, bf16),
        ],
        in_specs=[VMEM] * (groups + 2),
        out_specs=[HBM, VMEM, HBM],
        scratch_shapes=[
            pltpu.VMEM((tiles, own, LANES), bf16),
            pltpu.SemaphoreType.DMA(((kept.shape[0] + rest.shape[0]) // SPLIT,)),
            pltpu.SemaphoreType.DMA((rest.shape[0],)),
        ],
        compiler_params=params(16),
        name="project_first",
    )(*[onchip(p) for p in parts], onchip(kept), onchip(rest))


def project_next(anchor, pieces, kept, rest, me):
    slices, voxels = anchor.shape
    own = 8
    count = len(pieces)
    tiles = (kept.shape[0] + rest.shape[0]) * (slices // own) * kept.shape[1] // LANES

    def kernel(anchor_ref, *refs):
        piece_refs, rest_refs = refs[:count], refs[count:]
        kept_ref, rest_ref, out_ref, own_ref, gradient_ref, tile_ref, out_sems = rest_refs
        gradient = piece_refs[0][...]
        for ref in piece_refs[1:]:
            gradient = gradient + ref[...].astype(f32)
        gradient_ref[...] = gradient
        low = (anchor_ref[...] - 0.5 * gradient).astype(bf16)
        own_ref[...] = gradient_ref[pl.ds(pl.multiple_of(me() * own, own), own), :]
        for copy in project_tiles(low, piece_list(kept_ref, rest_ref), tile_ref, out_ref, out_sems):
            copy.wait()

    return pl.pallas_call(
        kernel,
        out_shape=[
            pltpu.HBM((tiles, own, LANES), bf16),
            jax.ShapeDtypeStruct((own, voxels), f32),
        ],
        in_specs=[VMEM] * (count + 3),
        out_specs=[HBM, VMEM],
        scratch_shapes=[
            pltpu.VMEM((slices, voxels), f32),
            pltpu.VMEM((tiles, own, LANES), bf16),
            pltpu.SemaphoreType.DMA(((kept.shape[0] + rest.shape[0]) // SPLIT,)),
        ],
        compiler_params=params(16),
        name="project_next",
    )(onchip(anchor), *[onchip(p) for p in pieces], onchip(kept), onchip(rest))


def back_project(misfit, kept, main, me, groups, whole):
    rows, voxels = kept.shape[1:]
    own = misfit.shape[1]
    blocks = rows // LANES

    def kernel(misfit_ref, kept_ref, main_ref, *refs):
        *outs, rest_ref, sems = refs if whole else refs[:-3] + refs[-2:]
        copies = [None] * KEPT + fetch(main_ref, rest_ref, sems)
        total = None
        for n, (ref, i) in enumerate(piece_list(kept_ref, rest_ref)):
            left = jnp.concatenate(
                [
                    jnp.concatenate(
                        [
                            misfit_ref[(n // SPLIT * groups + g) * (SPLIT * blocks) + n % SPLIT * blocks + j].astype(f32)
                            for j in range(blocks)
                        ],
                        axis=1,
                    )
                    for g in range(groups)
                ],
                axis=0,
            ).astype(bf16)
            if copies[n] is not None:
                copies[n].wait()
            part = jnp.dot(left, ref[i], preferred_element_type=f32)
            total = part if total is None else total + part
        if whole:
            outs[0][...] = total
            outs[1][...] = total.astype(bf16)
        else:
            total_ref = refs[-3]
            total_ref[...] = total
            for k in range(groups):
                first = pl.multiple_of(jnp.bitwise_xor(me(), k) * own, own)
                outs[k][...] = total_ref[pl.ds(first, own), :].astype(outs[k].dtype)

    if whole:
        outs = [jax.ShapeDtypeStruct((groups * own, voxels), t) for t in (f32, bf16)]
        outs.append(pltpu.VMEM(main.shape, bf16))
        scratch = []
    else:
        outs = [jax.ShapeDtypeStruct((own, voxels), f32 if k == 0 else bf16) for k in range(groups)]
        scratch = [pltpu.VMEM((groups * own, voxels), f32), pltpu.VMEM(main.shape, bf16)]
    return pl.pallas_call(
        kernel,
        out_shape=outs,
        in_specs=[VMEM, VMEM, HBM],
        out_specs=[VMEM] * len(outs),
        scratch_shapes=scratch + [pltpu.SemaphoreType.DMA((main.shape[0],))],
        compiler_params=params(16),
        name="back_project",
    )(onchip(misfit), onchip(kept), offchip(main))


def spread_misfit(half, other, sino, weight, copies):
    def kernel(half_ref, other_ref, sino_ref, weight_ref, out_ref):
        value = (weight_ref[...] * ((half_ref[...] + other_ref[...]) - sino_ref[...])).astype(bf16)
        for i in range(copies):
            out_ref[i] = value

    return pl.pallas_call(
        kernel,
        out_shape=jax.ShapeDtypeStruct((copies,) + half.shape, bf16),
        in_specs=[VMEM] * 4,
        out_specs=VMEM,
        compiler_params=params(4),
        name="spread_misfit",
    )(*[onchip(v) for v in (half, other, sino, weight)])


def halves(value):
    high = value.astype(bf16)
    return high, (value - high.astype(f32)).astype(bf16)


def product(weights, state_hi, state_lo):
    hi, lo = weights
    rows = hi.shape[0]
    both = jnp.dot(jnp.concatenate([hi, lo], axis=0), state_hi, preferred_element_type=f32)
    return both[:rows] + both[rows:] + jnp.dot(hi, state_lo, preferred_element_type=f32)


def denoise(low, own, high, first_in, middle, last_out, at, count, across):
    rows, width = PX, own.shape[1]
    depth, taps, hidden, _ = middle.shape
    step = taps * hidden // 3
    most = rows + 2 * (HALO - 1)
    tall = most + 2 + (-(most + 2)) % 8

    def kernel(low_ref, own_ref, high_ref, first_ref, mid_ref, last_ref, out_ref, hi_ref, lo_ref):
        lane = lax.broadcasted_iota(jnp.int32, (1, LANES), 1)
        not_first = (lane != 0).astype(f32)
        not_last = (lane != LANES - 1).astype(f32)

        def shifted(value):
            left, right = [], []
            for b in range(width // LANES):
                piece = value[:, b * LANES : (b + 1) * LANES]
                left.append(pltpu.roll(piece, 1, 1) * not_first)
                right.append(pltpu.roll(piece, LANES - 1, 1) * not_last)
            return jnp.concatenate(left, axis=1), value, jnp.concatenate(right, axis=1)

        def keep(layer, row, values):
            reach = HALO - 1 - layer
            index = at() * rows + (row - reach)
            inside = (index >= 0) & (index < count * rows)
            state = jnp.maximum(values, 0.0) * inside.astype(f32)
            for e, moved in enumerate(shifted(state)):
                at_row = step * row + hidden * e
                hi, lo = halves(moved)
                hi_ref[at_row : at_row + hidden, :] = hi
                lo_ref[at_row : at_row + hidden, :] = lo

        def banded(blocks, outs):
            blank = lambda n: [jnp.zeros((blocks[0].shape[0], n), f32)] if n else []
            return jnp.concatenate(
                [
                    jnp.concatenate(blank(step * i) + blocks + blank(step * (outs - 1 - i)), axis=1)
                    for i in range(outs)
                ],
                axis=0,
            )

        def turned(tiles):
            turn = jnp.swapaxes(jnp.stack(tiles), 0, 1)
            return jnp.concatenate([turn[b] for b in range(turn.shape[0])], axis=1)

        def cut(value):
            return [value[:, i : i + LANES] for i in range(0, value.shape[1], LANES)]

        spare = tall - rows - 2 * HALO
        if across:
            tiles = cut(low_ref[...]) + cut(own_ref[...]) + cut(high_ref[...])
            field = turned(tiles + [jnp.zeros_like(tiles[0])] * spare)
        else:
            field = jnp.concatenate(
                [low_ref[...], own_ref[...], high_ref[...], jnp.zeros((spare, width), f32)], axis=0
            )

        square = jnp.concatenate([first_ref[...], jnp.zeros((taps, LANES - hidden), f32)], axis=1)
        square = jnp.concatenate([square, jnp.zeros((LANES - taps, LANES), f32)], axis=0)
        first_taps = square.T[:hidden]
        shape = (most, hidden, 3 * tall)
        out_row = lax.broadcasted_iota(jnp.int32, shape, 0)
        column = lax.broadcasted_iota(jnp.int32, shape, 2)
        spread = jnp.zeros(shape, f32)
        for tap in range(9):
            a, e = tap // 3, tap % 3
            chosen = column == out_row + (a + e * tall)
            spread = jnp.where(chosen, first_taps[:, tap : tap + 1][None], spread)
        spread = spread.reshape(most * hidden, 3 * tall)

        state_hi, state_lo = halves(jnp.concatenate(shifted(field), axis=0))
        values = product(halves(spread), state_hi, state_lo)
        live = most
        for r in range(live):
            keep(0, r, values[hidden * r : hidden * (r + 1)])
        for layer in range(depth):
            weights = halves(banded([mid_ref[layer, t] for t in range(taps)], 3))
            live -= 2
            for r in range(0, live, 3):
                take = min(3, live - r)
                used = step * (take + 2)
                chunk = [w[: hidden * take, :used] for w in weights]
                state_hi = hi_ref[step * r : step * r + used, :]
                state_lo = lo_ref[step * r : step * r + used, :]
                values = product(chunk, state_hi, state_lo)
                for i in range(take):
                    keep(layer + 1, r + i, values[hidden * i : hidden * (i + 1)])
        used = step * live
        weights = halves(banded([last_ref[t : t + 1, :] for t in range(taps)], rows))
        change = product(weights, hi_ref[:used, :], lo_ref[:used, :])
        out_ref[...] = own_ref[...] - (turned(cut(change)) if across else change)

    return pl.pallas_call(
        kernel,
        out_shape=jax.ShapeDtypeStruct((rows, width), f32),
        in_specs=[VMEM] * 6,
        out_specs=VMEM,
        scratch_shapes=[pltpu.VMEM((most * step, width), bf16)] * 2,
        compiler_params=params(24),
        name="denoise",
    )(*[onchip(v) for v in (low, own, high, first_in, middle, last_out)])


def line(count, shift):
    return [(i, i + shift) for i in range(count) if 0 <= i + shift < count]


def swap(value, count, k, axis="agent"):
    return lax.ppermute(value, axis, [(i, i ^ k) for i in range(count)])


def join(model_state, planar_state, sagittal_state, gradient, pieces, planar_image, sagittal_image):
    count = len(pieces)

    def kernel(*refs):
        model, plane, side, first, plane_image, side_image = [r[...] for r in refs[:6]]
        piece_refs, outs = refs[6 : 6 + count], refs[6 + count :]
        second = piece_refs[0][...]
        for ref in piece_refs[1:]:
            second = second + ref[...].astype(f32)
        guess = model - 0.5 * first
        model_image = guess - 0.5 * (second + (guess - model))
        reflect_model = 2.0 * model_image - model
        reflect_plane = 2.0 * plane_image - plane
        reflect_side = 2.0 * side_image - side
        consensus = 0.5 * reflect_model + 0.25 * reflect_plane + 0.25 * reflect_side
        outs[0][0] = 0.5 * model + 0.5 * (2.0 * consensus - reflect_model)
        outs[1][0] = 0.5 * plane + 0.5 * (2.0 * consensus - reflect_plane)
        outs[2][0] = 0.5 * side + 0.5 * (2.0 * consensus - reflect_side)

    values = (model_state, planar_state, sagittal_state, gradient, planar_image, sagittal_image, *pieces)
    return pl.pallas_call(
        kernel,
        out_shape=[jax.ShapeDtypeStruct((1,) + model_state.shape, f32)] * 3,
        in_specs=[VMEM] * len(values),
        out_specs=[VMEM] * 3,
        compiler_params=params(4),
        name="join",
    )(*[onchip(v) for v in values])


def body(
    view_tile,
    block_mask,
    sinogram,
    bin_weight,
    model_state,
    planar_state,
    sagittal_state,
    planar_in,
    planar_mid,
    planar_out,
    sagittal_in,
    sagittal_mid,
    sagittal_out,
):
    agents = lax.axis_size("agent")
    tiles = lax.axis_size(TILE)
    spread = lax.axis_size(PLANE)
    spot = lax.axis_index(PLANE)
    own = model_state.shape[1]
    views, _, bins, _ = view_tile.shape
    per = views * agents * (bins // LANES) // spread
    agent = lambda: lax.axis_index("agent")
    tile_at = lambda: lax.axis_index(TILE)
    model_state, planar_state, sagittal_state = model_state[0], planar_state[0], sagittal_state[0]

    def share(values):
        tiled = values.reshape(views, agents, own, bins // LANES, LANES).transpose(0, 1, 3, 2, 4)
        return lax.dynamic_index_in_dim(tiled.reshape(spread, per, own, LANES), spot, 0, keepdims=False)

    def gathered(sent, shares):
        got = lax.all_to_all(sent.reshape(spread, per, own, LANES), PLANE, 0, 0)
        half = got.astype(f32).sum(axis=0)
        if shares is None:
            _, *whole = lax.optimization_barrier((half, sinogram, bin_weight))
            shares = [share(values) for values in whole]
        other = lax.ppermute(half, "zh", [(0, 1), (1, 0)])
        spreaded = spread_misfit(half, other, *shares, spread)
        misfit = lax.all_to_all(spreaded, PLANE, 0, 0)
        return misfit.reshape(spread * per, own, LANES), shares, half

    parts = [model_state] + [swap(model_state, agents, k) for k in range(1, agents)]
    kept, rest = mask_blocks(view_tile, block_mask.transpose(0, 2, 1, 3))
    sent, anchor, main = project_first(parts, kept, rest, agent)

    edge = HALO * LANES
    sent, plane, side = lax.optimization_barrier((sent, planar_state, sagittal_state))
    begin, end = plane[:, :edge], plane[:, -edge:]
    ends = spot == spread - 1
    pairs = [(spread - 1, 2 * spread - 1), (spread, 0)]
    across = lax.ppermute(jnp.where(ends, end, begin), TILE, pairs)
    misfit, shares, half = gathered(sent, None)
    _, begin, end = lax.optimization_barrier((half, begin, end))
    upper = lax.axis_index("zh") == 1
    blank = jnp.zeros_like(begin)
    up = jnp.where(ends, jnp.where(upper, across, blank), end)
    down = jnp.where(spot == 0, jnp.where(upper, blank, across), begin)
    plane_low = lax.ppermute(up, PLANE, [(i, (i + 1) % spread) for i in range(spread)])
    plane_high = lax.ppermute(down, PLANE, [((i + 1) % spread, i) for i in range(spread)])
    side_low = lax.ppermute(side[-HALO:], "agent", line(agents, 1))
    side_high = lax.ppermute(side[:HALO], "agent", line(agents, -1))

    total, piece, rest = back_project(misfit, kept, main, agent, agents, True)
    pieces = [total] + [swap(piece, agents, k) for k in range(1, agents)]
    sent, gradient = project_next(anchor, pieces, kept, rest, agent)
    misfit, *_ = gathered(sent, shares)
    pieces = back_project(misfit, kept, main, agent, agents, False)
    pieces = [pieces[0]] + [swap(pieces[k], agents, k) for k in range(1, agents)]
    kernels = (planar_in, planar_mid, planar_out)
    planar_image = denoise(plane_low, planar_state, plane_high, *kernels, tile_at, tiles, True)
    kernels = (sagittal_in, sagittal_mid, sagittal_out)
    sagittal_image = denoise(side_low, sagittal_state, side_high, *kernels, agent, agents, False)
    states = (model_state, planar_state, sagittal_state)
    return join(*states, gradient, pieces, planar_image, sagittal_image)


def solution(mesh):
    fine = Mesh(mesh.devices.reshape(2, 4, 4, 2, 4), TILE + ("agent",))
    return jax.shard_map(
        body,
        mesh=fine,
        in_specs=(
            P("agent", TILE, None, None),
            P("agent", TILE, None, None),
            P("agent", None, None),
            P("agent", None, None),
            P(TILE, "agent", None),
            P(TILE, "agent", None),
            P(TILE, "agent", None),
            P(),
            P(),
            P(),
            P(),
            P(),
            P(),
        ),
        out_specs=(P(TILE, "agent", None),) * 3,
        check_vma=False,
    )
```
